128 devices in a mesh: ctx: 4 (over z_lo, core), tp: 16 (over y, x), dp: 2 (over z_hi).
Axes of the slice: x: 4, y: 4, z: 4 (z_hi: 2, z_lo: 2; z = z_hi * 2 + z_lo), core: 2. Of those that a mesh axis runs over, the one named last changes fastest.
Arguments:
- hidden_in: bfloat16 [8192, 8192], P(('dp', 'ctx', 'tp')), parts along dimension 0
- norm_gain: float32 [8192], replicated
- q_weight: bfloat16 [8192, 8192], P(None, 'tp')
- kv_weight: bfloat16 [8192, 2048], P(None, 'tp')
- out_weight: bfloat16 [8192, 8192], P('tp'), may hold values from -0.25 to 0.25
- doc_lengths: int32 [16], P('dp'), parts along dimension 0, may hold values from 1 to 2048, 4096 in all
Outputs:
- attn_out: bfloat16 [8192, 8192], P(('dp', 'ctx', 'tp')), parts along dimension 0
The draws below stay inside these ranges and needn't reach their ends.
There are 2 independent parts, one for each index of `dp`. The reference program is written for one: setup_inputs(seed, part) draws one part's arguments, and reference() takes and returns one part's arrays. A program takes and returns all parts, laid end to end along the dimension named above; an argument that names none is the same for every part. Nothing has to cross between parts.
Inputs may be any that keep to these rules, and one draw needn't show every extreme that they name: `doc_lengths`: the lengths of a row sum to 4096; the longest document has exactly 2048 tokens.
All inputs are finite; a program needn't handle non-finite values.
Results may differ from the reference program's by a relative error of at most 0.015.
The reference program's roundings to bfloat16 on the way (of `normed`, `keys`, `weights` and `heads_out`) count: a program that leaves them out, or rounds other values in their place, can miss the bound.
Values may be sent and summed in bfloat16 or wider, within the bound.
No kernel may reach another device: no remote copies, remote signals or barrier semaphores. Data moves between devices by JAX's collectives and lax.ppermute only.
A program may use at most 128 MiB of HBM per device.

```python
import math
import jax
import jax.numpy as jnp
import numpy as np
from jax import lax

D = 8192
QH = 64
KVH = 8
HD = 128
L = 4096
DOCS = 8
MOST = 2048
N_TP = 16


def sink_feature():
    return 5 * D // 8 + 1


def sink_pattern(key):
    signs = jax.random.randint(jax.random.fold_in(key, 7101), (KVH, HD), 0, 2).astype(jnp.float32) * 2.0 - 1.0
    half = HD // 2
    planted = (jnp.arange(HD) % half >= half - half // 4).astype(jnp.float32)
    return signs * planted[None, :]


def base_weight(key, rows, cols):
    values = jax.random.truncated_normal(key, -4.0, 4.0, (rows, cols), jnp.float32)
    return values * rows ** (-0.5)


def drawn_row(base, row):
    marker = (jnp.arange(base.shape[0]) == sink_feature()).astype(jnp.float32)
    return base + marker[:, None] * row[None, :]


def width_scale():
    return math.sqrt(D * math.sqrt(HD))


def draw_q_weight(key, part):
    base = base_weight(jax.random.fold_in(key, 11), D, QH * HD)
    strength = jax.random.uniform(jax.random.fold_in(key, 7102), (QH,), jnp.float32, 250.0, 550.0)
    pattern = jnp.repeat(sink_pattern(key), QH // KVH, axis=0)
    per_head = pattern * (strength / (2.0 * width_scale()))[:, None]
    return drawn_row(base, per_head.reshape(QH * HD)).astype(jnp.bfloat16)


def draw_kv_weight(key, part):
    base = base_weight(jax.random.fold_in(key, 12), D, 2 * KVH * HD)
    key_row = sink_pattern(key).reshape(KVH * HD) * (8.0 / width_scale())
    row = jnp.concatenate([key_row, jnp.zeros((KVH * HD,), jnp.float32)])
    return drawn_row(base, row).astype(jnp.bfloat16)


def draw_norm_gain(key, part):
    gains = jnp.exp(jax.random.uniform(jax.random.fold_in(key, 13), (D,), jnp.float32, math.log(0.5), math.log(2.0)))
    near_one = jax.random.uniform(jax.random.fold_in(key, 14), (D,), jnp.float32, 0.9, 1.1)
    marker = jnp.arange(D) == sink_feature()
    return jnp.where(marker, near_one, gains)


def draw_hidden_in(key, part):
    base = jax.random.truncated_normal(jax.random.fold_in(key, 22), -6.0, 6.0, (L, D), jnp.float32)
    pair_count = L // 2
    chosen = jax.random.randint(jax.random.fold_in(key, 23), (pair_count,), 0, 16) == 0
    forced = jnp.arange(pair_count) == jax.random.randint(jax.random.fold_in(key, 24), (), 0, pair_count)
    strength = jax.random.uniform(jax.random.fold_in(key, 25), (pair_count,), jnp.float32, 2.5, 4.0) * math.sqrt(D)
    sink_rows = jnp.repeat(chosen | forced, 2)
    sink_values = jnp.repeat(strength, 2)
    column = jnp.arange(D) == sink_feature()
    return jnp.where(sink_rows[:, None] & column[None, :], sink_values[:, None], base).astype(jnp.bfloat16)


def steps_of(stream_key, extent, pieces, low, high):
    factor_of, own = 1.0, jax.random.fold_in(stream_key, 6)
    for axis_at, parts in pieces:
        steps = jnp.exp(jax.random.uniform(jax.random.fold_in(own, axis_at), (parts,), jnp.float32, low / len(pieces), high / len(pieces)))
        factor_of = factor_of * jnp.repeat(steps, extent[axis_at] // parts).reshape([-1 if axis == axis_at else 1 for axis in range(len(extent))])
    return factor_of


def profile(number_of, total, reach, slope):
    weights = [(1 << 20) // math.isqrt(grade ** slope) + 1 for grade in range(2, number_of + 1)]
    rest, holding = total - reach - (number_of - 1), [1] * (number_of - 1)
    while rest > 0:
        candidates = [i for i in range(number_of - 1) if holding[i] < reach]
        whole, remaining = sum([weights[i] for i in candidates]), rest
        for i in candidates:
            extra = min(reach - holding[i], max(1, remaining * weights[i] // whole), rest)
            holding[i] = holding[i] + extra
            rest = rest - extra
    return np.array([reach] + holding)


def uneven(rng, number_of, total, reach, skew):
    if number_of == 2:
        one = jax.random.randint(rng, (), max(1, total - reach), min(reach, total - 1) + 1)
        return jnp.stack([one, total - one])
    tallies = jnp.asarray(profile(number_of, total, reach, skew), jnp.int32)
    couples = (number_of - 1) // 2
    source_of, taker = tallies[1:1 + 2 * couples:2], tallies[2:2 + 2 * couples:2]
    room = jnp.minimum(source_of - 1, reach - taker)
    moved = jax.random.randint(jax.random.fold_in(rng, 1), (couples,), 0, 1 << 20) % (room + 1)
    tallies = tallies.at[1:1 + 2 * couples:2].set(source_of - moved).at[2:2 + 2 * couples:2].set(taker + moved)
    return tallies[jax.random.permutation(jax.random.fold_in(rng, 2), number_of)]


def scatter_about(rng, extent, width, limit, pieces=(), kind=jnp.bfloat16):
    level = steps_of(rng, extent, pieces, -0.22, 0.18) if pieces else 1.0
    values = jax.random.normal(rng, extent, jnp.float32) * width * level
    return jnp.minimum(jnp.maximum(values, -limit), limit).astype(kind)


def setup_inputs(seed: int = 0, part: int = 0) -> dict:
    key_list = jax.random.split(jax.random.key(seed), 7)
    part_splits = jax.random.split(jax.random.fold_in(key_list[6], part), 7)
    hidden_in = draw_hidden_in(jax.random.fold_in(jax.random.fold_in(key_list[6], part), 71), part)
    norm_gain = draw_norm_gain(jax.random.fold_in(key_list[6], 71), part)
    q_weight = draw_q_weight(jax.random.fold_in(key_list[6], 71), part)
    kv_weight = draw_kv_weight(jax.random.fold_in(key_list[6], 71), part)
    out_weight = scatter_about(key_list[4], (QH * HD, D), (QH * HD // 16) ** -0.5, 0.25, ((0, 16),))
    doc_lengths = uneven(part_splits[5], DOCS, L, MOST, 2).astype(jnp.int32)
    return {"hidden_in": hidden_in, "norm_gain": norm_gain, "q_weight": q_weight, "kv_weight": kv_weight, "out_weight": out_weight, "doc_lengths": doc_lengths}


def doc_index(positions, ends):
    return lax.optimization_barrier(jnp.sum((positions[:, None] >= ends[None, :]).astype(jnp.int32), axis=1)).astype(jnp.int32)

def doc_start(positions, lengths, ends):
    return lax.optimization_barrier(jnp.sum(jnp.where(positions[:, None] >= ends[None, :], lengths[None, :], 0), axis=1)).astype(jnp.int32)

def rope_freqs(half):
    base = jnp.power(jnp.float32(500000.0), -(jnp.arange(half, dtype=jnp.float32) * 2.0) / HD)
    wavelen = 2.0 * math.pi / base
    smooth = (8192.0 / wavelen - 1.0) / 3.0
    middle = (1.0 - smooth) * base / 8.0 + smooth * base
    return jnp.where(wavelen < 2048.0, base, jnp.where(wavelen > 8192.0, base / 8.0, middle))

def rotate(values, within):
    rows = values.shape[0]
    blocks = values.reshape(rows, values.shape[1] // HD, HD)
    half = HD // 2
    freqs = rope_freqs(half)
    angles = within.astype(jnp.float32)[:, None] * freqs[None, :]
    cosine = jnp.cos(angles)[:, None, :]
    sine = jnp.sin(angles)[:, None, :]
    first = blocks[:, :, :half]
    second = blocks[:, :, half:]
    turned = jnp.concatenate([first * cosine - second * sine, second * cosine + first * sine], axis=2)
    return turned.reshape(rows, values.shape[1])

def reference(hidden_in, norm_gain, q_weight, kv_weight, out_weight, doc_lengths):
    x = hidden_in.astype(jnp.float32)
    normed = (x * lax.rsqrt(lax.optimization_barrier(jnp.mean(x * x, axis=1, keepdims=True)) + 1e-05) * norm_gain[None, :]).astype(jnp.bfloat16)
    ends = jnp.cumsum(doc_lengths).astype(jnp.int32)
    positions = jnp.arange(L, dtype=jnp.int32)
    docs = doc_index(positions, ends)
    within = positions - doc_start(positions, doc_lengths, ends)
    q_raw = jnp.dot(normed, q_weight, preferred_element_type=jnp.float32)
    kv_raw = jnp.dot(normed, kv_weight, preferred_element_type=jnp.float32)
    queries = rotate(q_raw, within).astype(jnp.bfloat16)
    keys = rotate(kv_raw[:, :KVH * HD], within).astype(jnp.bfloat16)
    values = kv_raw[:, KVH * HD:].astype(jnp.bfloat16)
    q_heads = queries.reshape(L, QH, HD).transpose(1, 0, 2)
    k_heads = keys.reshape(L, KVH, HD).transpose(1, 0, 2)
    v_heads = values.reshape(L, KVH, HD).transpose(1, 0, 2)
    visible = (docs[None, :] == docs[:, None]) & (positions[None, :] <= positions[:, None])
    group = QH // KVH
    scale = HD ** (-0.5)

    def one_head(head):
        kv_head = head // group
        q_one = lax.dynamic_index_in_dim(q_heads, head, 0, keepdims=False)
        k_one = lax.dynamic_index_in_dim(k_heads, kv_head, 0, keepdims=False)
        v_one = lax.dynamic_index_in_dim(v_heads, kv_head, 0, keepdims=False)
        scores = jnp.dot(q_one, k_one.T, preferred_element_type=jnp.float32) * scale
        scores = jnp.where(visible, scores, jnp.float32(-1e+30))
        top = lax.optimization_barrier(jnp.max(scores, axis=1, keepdims=True))
        expd = jnp.where(visible, jnp.exp(scores - top), jnp.float32(0.0))
        total = lax.optimization_barrier(jnp.sum(expd, axis=1, keepdims=True))
        summed = jnp.dot(expd.astype(jnp.bfloat16), v_one, preferred_element_type=jnp.float32)
        return (summed / total).astype(jnp.bfloat16)
    heads_out = lax.map(one_head, jnp.arange(QH, dtype=jnp.int32))
    heads_out = heads_out.transpose(1, 0, 2).reshape(L, QH * HD)
    cols = QH * HD // N_TP
    grouped = heads_out.reshape(L, N_TP, cols).transpose(1, 0, 2)
    weights_grouped = out_weight.reshape(N_TP, cols, D)

    def add_group(total, pair):
        term = jnp.dot(pair[0], pair[1], preferred_element_type=jnp.float32).astype(jnp.bfloat16)
        term = lax.optimization_barrier(term)
        return (total + term.astype(jnp.float32), None)
    summed, unused = lax.scan(add_group, jnp.zeros((L, D), jnp.float32), (grouped, weights_grouped))
    return summed.astype(jnp.bfloat16)
```

```python
import functools
import math

import jax
import jax.numpy as jnp
from jax import lax
from jax.experimental import pallas as pl
from jax.experimental.pallas import tpu as pltpu
from jax.sharding import PartitionSpec as P

QH = 64
KVH = 8
HD = 128


def from_everyone(shard, axis):
    length = lax.axis_size(axis)
    return lax.all_to_all(
        jnp.broadcast_to(shard[None], (length, *shard.shape)), axis, 0, 0, tiled=True
    )


def laid_out(blocks, dim):
    blocks = jnp.moveaxis(blocks, 0, dim)
    shape = blocks.shape
    return blocks.reshape(*shape[:dim], shape[dim] * shape[dim + 1], *shape[dim + 2 :])


def gathered_copies(shard, axis, dim):
    blocks = from_everyone(shard, axis)
    return laid_out(blocks, dim)


def doc_start(positions, lengths, ends):
    return jnp.sum(jnp.where(positions[:, None] >= ends[None, :], lengths[None, :], 0), axis=1)


def rope_freqs(half):
    base = jnp.power(jnp.float32(500000.0), -(jnp.arange(half, dtype=jnp.float32) * 2.0) / HD)
    wavelen = 2.0 * math.pi / base
    smooth = (8192.0 / wavelen - 1.0) / 3.0
    middle = (1.0 - smooth) * base / 8.0 + smooth * base
    return jnp.where(wavelen < 2048.0, base, jnp.where(wavelen > 8192.0, base / 8.0, middle))


def rotate(values, within):
    rows = values.shape[0]
    blocks = values.reshape(rows, values.shape[1] // HD, HD)
    half = HD // 2
    freqs = rope_freqs(half)
    angles = within.astype(jnp.float32)[:, None] * freqs[None, :]
    cosine = jnp.cos(angles)[:, None, :]
    sine = jnp.sin(angles)[:, None, :]
    first = blocks[:, :, :half]
    second = blocks[:, :, half:]
    turned = jnp.concatenate(
        [first * cosine - second * sine, second * cosine + first * sine], axis=2
    )
    return turned.reshape(rows, values.shape[1])


def attn_kernel(heads, bq, bk, docs, info_ref, q_ref, k_ref, v_ref, o_ref, acc_ref):
    first = info_ref[0] + pl.program_id(0) * bq
    last = first + bq - 1
    rows = first + lax.broadcasted_iota(jnp.int32, (1, bq), 1)
    low = jnp.zeros((1, bq), jnp.int32)
    low_first = jnp.int32(0)
    for d in range(docs):
        end = info_ref[1 + d]
        low = jnp.where(rows >= end, jnp.maximum(low, end), low)
        low_first = jnp.where(first >= end, jnp.maximum(low_first, end), low_first)
    factor = HD ** (-0.5) * math.log2(math.e)
    acc_ref[...] = jnp.zeros_like(acc_ref)

    def step(i, state):
        at = pl.multiple_of(i * bk, bk)
        key = k_ref[pl.ds(at, bk), :]
        value = v_ref[pl.ds(at, bk), :]
        index = at + lax.broadcasted_iota(jnp.int32, (bk, 1), 0)
        visible = (index >= low) & (index <= rows)
        out = []
        for h in range(heads):
            top, total = state[h]
            scores = lax.dot_general(
                key, q_ref[:, h * HD : (h + 1) * HD], (((1,), (1,)), ((), ())), preferred_element_type=jnp.float32
            )
            scores = jnp.where(visible, scores * factor, jnp.float32(-1e30))
            new = jnp.maximum(top, jnp.max(scores, axis=0, keepdims=True))
            keep = jnp.exp2(top - new)
            expd = jnp.exp2(scores - new)
            total = total * keep + jnp.sum(expd, axis=0, keepdims=True)
            acc_ref[h] = acc_ref[h] * keep + lax.dot_general(
                value, expd.astype(jnp.bfloat16), (((0,), (0,)), ((), ())), preferred_element_type=jnp.float32
            )
            out.append((new, total))
        return tuple(out)

    start = tuple((jnp.full((1, bq), -1e30, jnp.float32), jnp.zeros((1, bq), jnp.float32)) for _ in range(heads))
    state = lax.fori_loop(low_first // bk, last // bk + 1, step, start)
    for h in range(heads):
        o_ref[:, h * HD : (h + 1) * HD] = (acc_ref[h] / state[h][1]).T.astype(o_ref.dtype)

def attention(info, q, k, v, heads, bq=256, bk=256, docs=8):
    rows = q.shape[0]
    return pl.pallas_call(
        functools.partial(attn_kernel, heads, bq, bk, docs),
        grid_spec=pltpu.PrefetchScalarGridSpec(
            num_scalar_prefetch=1,
            grid=(rows // bq,),
            in_specs=[
                pl.BlockSpec((bq, heads * HD), lambda i, s: (i, 0)),
                pl.BlockSpec((k.shape[0], HD), lambda i, s: (0, 0)),
                pl.BlockSpec((v.shape[0], HD), lambda i, s: (0, 0)),
            ],
            out_specs=pl.BlockSpec((bq, heads * HD), lambda i, s: (i, 0)),
            scratch_shapes=[pltpu.VMEM((heads, HD, bq), jnp.float32)],
        ),
        out_shape=jax.ShapeDtypeStruct((rows, heads * HD), jnp.bfloat16),
        compiler_params=pltpu.CompilerParams(vmem_limit_bytes=40 * 2**20),
        name="attention",
    )(info, q, k, v)


def local(hidden_in, norm_gain, q_weight, kv_weight, out_weight, doc_lengths):
    tok_rows = hidden_in.shape[0]
    n_tp = lax.axis_size("tp")
    ctx_rows = tok_rows * n_tp
    q_cols = q_weight.shape[1]
    heads_here = q_cols // HD
    kv_cols = kv_weight.shape[1]
    tp_index = lax.axis_index("tp")
    ctx_index = lax.axis_index("ctx")
    x = hidden_in.astype(jnp.float32)
    normed = (
        x * lax.rsqrt(jnp.mean(x * x, axis=1, keepdims=True) + 1e-05) * norm_gain[None, :]
    ).astype(jnp.bfloat16)
    ends = jnp.cumsum(doc_lengths)
    is_key = tp_index * kv_cols < KVH * HD
    piece = lax.all_gather(normed, "tp", axis=0, tiled=True)
    count = piece.shape[0]
    positions = ctx_index * ctx_rows + jnp.arange(count, dtype=jnp.int32)
    within = positions - doc_start(positions, doc_lengths, ends)
    q_raw = jnp.dot(piece, q_weight, preferred_element_type=jnp.float32)
    kv_raw = jnp.dot(piece, kv_weight, preferred_element_type=jnp.float32)
    q_done = rotate(q_raw, within).astype(jnp.bfloat16)
    kv_done = jnp.where(is_key, rotate(kv_raw, within), kv_raw).astype(jnp.bfloat16)
    projected = jnp.concatenate([q_done, kv_done], axis=1)
    queries = projected[:, :q_cols]
    kv_part = projected[:, q_cols:]
    half = lax.axis_size("tp") // 2
    same = [(i, 2 * i) for i in range(half)] + [(half + i, 2 * i + 1) for i in range(half)]
    other = [(i, 2 * i + 1) for i in range(half)] + [(half + i, 2 * i) for i in range(half)]
    one = lax.ppermute(kv_part, "tp", same)
    two = lax.ppermute(kv_part, "tp", other)
    even = tp_index % 2 == 0
    kv_mine = jnp.concatenate([jnp.where(even, one, two), jnp.where(even, two, one)], axis=1)
    piece = gathered_copies(kv_mine, "ctx", 0)
    info = jnp.concatenate([(ctx_index * ctx_rows)[None], ends]).astype(jnp.int32)
    heads_out = attention(info, queries, piece[:, :HD], piece[:, HD:], heads_here, docs=doc_lengths.shape[0])
    return lax.psum_scatter(
        jnp.dot(heads_out, out_weight, preferred_element_type=jnp.float32).astype(jnp.bfloat16),
        "tp",
        scatter_dimension=0,
        tiled=True,
    )


def solution(mesh):
    placed = (
        P(("dp", "ctx", "tp"), None),
        P(),
        P(None, "tp"),
        P(None, "tp"),
        P("tp", None),
        P("dp"),
    )
    return jax.shard_map(
        local, mesh=mesh, in_specs=placed, out_specs=P(("dp", "ctx", "tp"), None), check_vma=False
    )
```

```python
import functools
import math

import jax
import jax.numpy as jnp
from jax import lax
from jax.experimental import pallas as pl
from jax.experimental.pallas import tpu as pltpu
from jax.sharding import PartitionSpec as P


QH = 64
KVH = 8
HD = 128
INTERPRET = False
MIB = 2**20

ORDERS = ((1, 3, 4, 12), (3, 1, 12, 4), (4, 12, 1, 3), (12, 4, 3, 1))
COLOURS = len(ORDERS)
SUB = 16


def swap(value, axis, mask):
    size = lax.axis_size(axis)
    return lax.ppermute(value, axis, [(i, i ^ mask) for i in range(size)])


def mask_of(order, place):
    mask = 0
    for bit, step in enumerate(order):
        if place >> bit & 1:
            mask ^= step
    return mask


def doc_start(positions, ends):
    return jnp.max(jnp.where(positions[:, None] >= ends[None, :], ends[None, :], 0), axis=1)


def rope_freqs(half):
    base = jnp.power(jnp.float32(500000.0), -(jnp.arange(half, dtype=jnp.float32) * 2.0) / HD)
    wavelen = 2.0 * math.pi / base
    smooth = (8192.0 / wavelen - 1.0) / 3.0
    middle = (1.0 - smooth) * base / 8.0 + smooth * base
    return jnp.where(wavelen < 2048.0, base, jnp.where(wavelen > 8192.0, base / 8.0, middle))


def rope_tables(positions, ends):
    within = positions - doc_start(positions, ends)
    angles = within.astype(jnp.float32)[:, None] * rope_freqs(HD // 2)[None, :]
    cosine, sine = jnp.cos(angles), jnp.sin(angles)
    return jnp.concatenate([cosine, cosine], axis=1), jnp.concatenate([-sine, sine], axis=1)


def project_kernel(places, turned, info_ref, *refs):
    xs, (w_ref, cos_ref, sin_ref) = refs[:COLOURS], refs[COLOURS : COLOURS + 3]
    prev_ref = refs[COLOURS + 3] if places else None
    out_ref, acc_ref = refs[-2:]
    step = pl.program_id(0)
    x = jnp.concatenate([ref[...] for ref in xs], axis=0)
    term = jnp.dot(x, w_ref[...], preferred_element_type=jnp.float32)

    @pl.when(step == 0)
    def _():
        acc_ref[...] = term

    @pl.when(step > 0)
    def _():
        acc_ref[...] += term

    @pl.when(step == pl.num_programs(0) - 1)
    def _():
        cosine, sine = cos_ref[...], sin_ref[...]
        for block in range(acc_ref.shape[1] // HD):
            cols = slice(block * HD, (block + 1) * HD)
            raw = acc_ref[:, cols]
            done = raw * cosine + pltpu.roll(raw, HD // 2, 1) * sine
            if not turned:
                done = jnp.where(info_ref[1] > 0, done, raw)
            done = done.astype(out_ref.dtype)
            if not places:
                out_ref[:, cols] = done
                continue
            for source, at, mask, row in places:
                rows = slice(at, at + SUB)
                dest = pl.multiple_of((info_ref[0] ^ mask) * (SUB * COLOURS) + row, SUB)
                out_ref[pl.ds(dest, SUB), cols] = done[rows] if source else prev_ref[rows, cols]


def project(info, xs, weight, tables, turned, prev=None, places=None, block=1024):
    rows, features = xs[0].shape
    cols = weight.shape[1]
    block = min(block, features)
    total = rows * COLOURS
    out_rows = 2 * total if places else total
    whole = lambda k, s: (0, 0)
    operands = [*xs, weight, *tables] + ([prev] if places else [])
    specs = [pl.BlockSpec((rows, block), lambda k, s: (0, k))] * COLOURS
    specs += [pl.BlockSpec((block, cols), lambda k, s: (k, 0))]
    specs += [pl.BlockSpec((total, HD), whole)] * 2
    specs += [pl.BlockSpec((total, cols), whole)] if places else []
    return pl.pallas_call(
        functools.partial(project_kernel, places, turned),
        grid_spec=pltpu.PrefetchScalarGridSpec(
            num_scalar_prefetch=1,
            grid=(features // block,),
            in_specs=specs,
            out_specs=pl.BlockSpec((out_rows, cols), whole),
            scratch_shapes=[pltpu.VMEM((total, cols), jnp.float32)],
        ),
        out_shape=jax.ShapeDtypeStruct((out_rows, cols), jnp.bfloat16),
        compiler_params=pltpu.CompilerParams(vmem_limit_bytes=24 * MIB),
        cost_estimate=pl.CostEstimate(
            flops=2 * total * features * cols,
            bytes_accessed=2 * features * (total + cols),
            transcendentals=0,
        ),
        name="project",
        interpret=INTERPRET,
    )(info, *operands)


def attention_kernel(heads, keys, docs, info_ref, q_ref, kv_ref, o_ref, acc_ref):
    width = q_ref.shape[0]
    part = kv_ref.shape[0] // 4
    first = info_ref[1] + pl.program_id(0) * width
    last = first + width - 1
    rows = first + lax.broadcasted_iota(jnp.int32, (1, width), 1)
    low = jnp.zeros((1, width), jnp.int32)
    low_first = jnp.int32(0)
    low_last = jnp.int32(0)
    for d in range(docs):
        end = info_ref[2 + d]
        low = jnp.where(rows >= end, jnp.maximum(low, end), low)
        low_first = jnp.where(first >= end, jnp.maximum(low_first, end), low_first)
        low_last = jnp.where(last >= end, jnp.maximum(low_last, end), low_last)
    factor = HD ** (-0.5) * math.log2(math.e)
    acc_ref[...] = jnp.zeros_like(acc_ref)

    def step(masked, i, state):
        begin = i * keys
        apart = (begin // part) ^ info_ref[0]
        at = pl.multiple_of(((apart >> 1) + (apart & 1) * 2) * part + begin % part, keys)
        key = kv_ref[pl.ds(at, keys), :HD]
        value = kv_ref[pl.ds(at, keys), HD:]
        if masked:
            index = begin + lax.broadcasted_iota(jnp.int32, (keys, 1), 0)
            visible = (index >= low) & (index <= rows)
        scored = [
            lax.dot_general(
                key, q_ref[:, h * HD : (h + 1) * HD], (((1,), (1,)), ((), ())), preferred_element_type=jnp.float32
            )
            for h in range(heads)
        ]
        out = []
        for h in range(heads):
            top, total = state[h]
            scores = scored[h] * factor
            if masked:
                scores = jnp.where(visible, scores, jnp.float32(-1e30))
            new = jnp.maximum(top, jnp.max(scores, axis=0, keepdims=True))
            keep = jnp.exp2(top - new)
            expd = jnp.exp2(scores - new)
            total = total * keep + jnp.sum(expd, axis=0, keepdims=True)
            acc_ref[h] = acc_ref[h] * keep + lax.dot_general(
                value, expd.astype(jnp.bfloat16), (((0,), (0,)), ((), ())), preferred_element_type=jnp.float32
            )
            out.append((new, total))
        return tuple(out)

    state = tuple((jnp.full((1, width), -1e30, jnp.float32), jnp.zeros((1, width), jnp.float32)) for _ in range(heads))
    begin, end = low_first // keys, last // keys + 1
    clear = jnp.minimum((low_last + keys - 1) // keys, end)
    edge = jnp.maximum(first // keys, clear)
    state = lax.fori_loop(begin, clear, functools.partial(step, True), state)
    state = lax.fori_loop(clear, edge, functools.partial(step, False), state)
    state = lax.fori_loop(edge, end, functools.partial(step, True), state)
    for h in range(heads):
        o_ref[:, h * HD : (h + 1) * HD] = (acc_ref[h] / state[h][1]).T.astype(o_ref.dtype)


def attention(info, q, kv, docs, width=256, keys=512):
    rows, cols = q.shape
    heads = cols // HD
    return pl.pallas_call(
        functools.partial(attention_kernel, heads, keys, docs),
        grid_spec=pltpu.PrefetchScalarGridSpec(
            num_scalar_prefetch=1,
            grid=(rows // width,),
            in_specs=[
                pl.BlockSpec((width, cols), lambda i, s: (i, 0)),
                pl.BlockSpec(kv.shape, lambda i, s: (0, 0)),
            ],
            out_specs=pl.BlockSpec((width, cols), lambda i, s: (i, 0)),
            scratch_shapes=[pltpu.VMEM((heads, HD, width), jnp.float32)],
        ),
        out_shape=jax.ShapeDtypeStruct((rows, cols), jnp.bfloat16),
        compiler_params=pltpu.CompilerParams(vmem_limit_bytes=40 * MIB),
        cost_estimate=pl.CostEstimate(
            flops=4 * rows * cols * 2048, bytes_accessed=8 * MIB, transcendentals=rows * heads * 2048
        ),
        name="attention",
        interpret=INTERPRET,
    )(info, q, kv)


def outward_kernel(masks, info_ref, h_ref, w_ref, keep_ref, send_ref, moved_ref):
    rows = h_ref.shape[0] // len(masks)

    @pl.when(pl.program_id(0) == 0)
    def _():
        for place, mask in enumerate(masks):
            source = pl.multiple_of((info_ref[0] ^ mask) * rows, rows)
            moved_ref[place * rows : (place + 1) * rows, :] = h_ref[pl.ds(source, rows), :]

    half = keep_ref.shape[0]
    weight = w_ref[...]
    send_ref[...] = jnp.dot(moved_ref[half:, :], weight, preferred_element_type=jnp.float32).astype(send_ref.dtype)
    keep_ref[...] = jnp.dot(moved_ref[:half, :], weight, preferred_element_type=jnp.float32).astype(keep_ref.dtype)


def outward(info, heads_out, weight, colour, masks, block=512):
    rows, inner = heads_out.shape
    cols = weight.shape[1] // COLOURS
    block = min(block, cols)
    steps = cols // block
    half = jax.ShapeDtypeStruct((rows // 2, cols), jnp.bfloat16)
    return pl.pallas_call(
        functools.partial(outward_kernel, masks),
        grid_spec=pltpu.PrefetchScalarGridSpec(
            num_scalar_prefetch=1,
            grid=(steps,),
            in_specs=[
                pl.BlockSpec((rows, inner), lambda n, s: (0, 0)),
                pl.BlockSpec((inner, block), lambda n, s: (0, colour * steps + n)),
            ],
            out_specs=[pl.BlockSpec((rows // 2, block), lambda n, s: (0, n))] * 2,
            scratch_shapes=[pltpu.VMEM((rows, inner), jnp.bfloat16)],
        ),
        out_shape=[half, half],
        compiler_params=pltpu.CompilerParams(vmem_limit_bytes=24 * MIB),
        cost_estimate=pl.CostEstimate(
            flops=2 * rows * inner * cols, bytes_accessed=2 * (rows * inner + inner * cols + rows * cols), transcendentals=0
        ),
        name="outward",
        interpret=INTERPRET,
    )(info, heads_out, weight)


def local(hidden_in, norm_gain, q_weight, kv_weight, out_weight, doc_lengths):
    tok_rows = hidden_in.shape[0]
    n_tp = lax.axis_size("tp")
    ctx_rows = tok_rows * n_tp
    tp_index = lax.axis_index("tp")
    ctx_index = lax.axis_index("ctx")
    x = hidden_in.astype(jnp.float32)
    normed = (
        x * lax.rsqrt(jnp.mean(x * x, axis=1, keepdims=True) + 1e-05) * norm_gain[None, :]
    ).astype(jnp.bfloat16)
    ends = jnp.cumsum(doc_lengths).astype(jnp.int32)
    first_row = ctx_index * ctx_rows

    held = [normed[c * SUB : (c + 1) * SUB] for c in range(COLOURS)]
    steps = len(ORDERS[0])
    for step in range(steps - 1):
        held = [jnp.concatenate([s, swap(s, "tp", ORDERS[c][step])], axis=0) for c, s in enumerate(held)]
    late = [swap(s, "tp", ORDERS[c][steps - 1]) for c, s in enumerate(held)]

    half = n_tp // 2
    tables = []
    places = []
    for part in range(2):
        starts = []
        for c, order in enumerate(ORDERS):
            for p in range(half):
                mask = mask_of(order, part * half + p)
                starts.append((tp_index ^ mask) * tok_rows + c * SUB)
                places.append((part, (c * half + p) * SUB, mask, c * SUB))
        positions = first_row + (jnp.stack(starts)[:, None] + jnp.arange(SUB)[None, :]).reshape(-1)
        tables.append(rope_tables(positions.astype(jnp.int32), ends))
    places = tuple(places)
    is_key = tp_index < n_tp // 2
    info = jnp.stack([tp_index, is_key.astype(jnp.int32)]).astype(jnp.int32)

    kv_early = project(info, held, kv_weight, tables[0], False)
    q_early = project(info, held, q_weight, tables[0], True)
    kv_part = project(info, late, kv_weight, tables[1], False, kv_early, places)
    same = [(i, 2 * i) for i in range(half)] + [(half + i, 2 * i + 1) for i in range(half)]
    other = [(i, 2 * i + 1) for i in range(half)] + [(half + i, 2 * i) for i in range(half)]
    one = lax.ppermute(kv_part, "tp", same)
    two = lax.ppermute(kv_part, "tp", other)
    even = tp_index % 2 == 0
    kv_mine = jnp.concatenate([jnp.where(even, one, two), jnp.where(even, two, one)], axis=1)
    kv_chip = jnp.concatenate([kv_mine, swap(kv_mine, "ctx", 2)], axis=0)
    kv_all = jnp.concatenate([kv_chip, swap(kv_chip, "ctx", 1)], axis=0)
    queries = project(info, late, q_weight, tables[1], True, q_early, places)

    where = jnp.concatenate([jnp.stack([ctx_index, first_row]).astype(jnp.int32), ends])
    heads_out = attention(where, queries, kv_all, doc_lengths.shape[0])

    kept, sent = [], []
    for c, order in enumerate(ORDERS):
        masks = tuple(mask_of(order[::-1], p) for p in range(n_tp))
        keep, send = outward(info, heads_out, out_weight, c, masks)
        kept.append(keep)
        sent.append(send)
    for step in range(steps):
        arrived = [swap(s, "tp", ORDERS[c][step]) for c, s in enumerate(sent)]
        sums = [(k.astype(jnp.float32) + a.astype(jnp.float32)).astype(jnp.bfloat16) for k, a in zip(kept, arrived)]
        rows = sums[0].shape[0] // 2
        kept = [s[:rows] for s in sums]
        sent = [s[rows:] for s in sums]
    return jnp.concatenate(sums, axis=1)


def solution(mesh):
    placed = (
        P(("dp", "ctx", "tp"), None),
        P(),
        P(None, "tp"),
        P(None, "tp"),
        P("tp", None),
        P("dp"),
    )
    return jax.shard_map(
        local, mesh=mesh, in_specs=placed, out_specs=P(("dp", "ctx", "tp"), None), check_vma=False
    )
```

```python
import functools
import math

import jax
import jax.numpy as jnp
from jax import lax
from jax.experimental import pallas as pl
from jax.experimental.pallas import tpu as pltpu
from jax.sharding import PartitionSpec as P


QH = 64
KVH = 8
HD = 128
INTERPRET = False
MIB = 2**20

GATHER = ((4, 12, 3), (12, 4, 3), (3, 4, 12), (3, 12, 4))
REDUCE = ((3, 4, 12), (3, 12, 4), (4, 12, 3), (12, 4, 3))
COLOURS = len(GATHER)
SUB = 16
COLUMN = ("ctx", "dp")
BELOW, AROUND, CORE = 4, 5, 2


def swap(value, axis, mask):
    size = math.prod(lax.axis_size(a) for a in ((axis,) if isinstance(axis, str) else axis))
    return lax.ppermute(value, axis, [(i, i ^ mask) for i in range(size)])


def mask_of(order, place):
    mask = 0
    for bit, step in enumerate(order):
        if place >> bit & 1:
            mask ^= step
    return mask


def place_of(mask):
    return (mask >> 2) * 2 + (mask & 1)


def after(value, *earlier):
    return lax.optimization_barrier((value, *earlier))[0]


def column_gather(piece):
    n = piece.shape[0] // 2
    first, second = piece[:n], piece[n:]
    first = jnp.concatenate([first, swap(first, COLUMN, BELOW)], axis=0)
    second = jnp.concatenate([second, swap(second, COLUMN, AROUND)], axis=0)
    near = jnp.concatenate([first, second], axis=0)
    far = jnp.concatenate([swap(first, COLUMN, AROUND), swap(second, COLUMN, BELOW)], axis=0)
    cross = BELOW ^ AROUND
    rows = {}
    for shift, (one, two) in enumerate(((near, far), (swap(near, COLUMN, CORE), swap(far, COLUMN, CORE)))):
        shift *= CORE
        for at, (source, left, right) in enumerate(((one, 0, 0), (one, BELOW, AROUND), (two, AROUND, BELOW), (two, cross, cross))):
            at = at % 2 * n
            rows[(left ^ shift, 0)] = source[at : at + n]
            rows[(right ^ shift, 1)] = source[2 * n + at : 3 * n + at]
    return jnp.concatenate([rows[(mask, side)] for mask in range(8) for side in range(2)], axis=0), far


def doc_start(positions, ends):
    return jnp.max(jnp.where(positions[:, None] >= ends[None, :], ends[None, :], 0), axis=1)


def rope_freqs(half):
    base = jnp.power(jnp.float32(500000.0), -(jnp.arange(half, dtype=jnp.float32) * 2.0) / HD)
    wavelen = 2.0 * math.pi / base
    smooth = (8192.0 / wavelen - 1.0) / 3.0
    middle = (1.0 - smooth) * base / 8.0 + smooth * base
    return jnp.where(wavelen < 2048.0, base, jnp.where(wavelen > 8192.0, base / 8.0, middle))


def rope_tables(positions, ends):
    within = positions - doc_start(positions, ends)
    angles = within.astype(jnp.float32)[:, None] * rope_freqs(HD // 2)[None, :]
    cosine, sine = jnp.cos(angles), jnp.sin(angles)
    return jnp.concatenate([cosine, cosine], axis=1), jnp.concatenate([-sine, sine], axis=1)


def project_kernel(pieces, turned, places, info_ref, *refs):
    xs, (w_ref, cos_ref, sin_ref, out_ref, acc_ref) = refs[:pieces], refs[pieces:]
    step = pl.program_id(0)
    x = jnp.concatenate([ref[...] for ref in xs], axis=0)
    term = jnp.dot(x, w_ref[...], preferred_element_type=jnp.float32)

    @pl.when(step == 0)
    def _():
        acc_ref[...] = term

    @pl.when(step > 0)
    def _():
        acc_ref[...] += term

    @pl.when(step == pl.num_programs(0) - 1)
    def _():
        cosine, sine = cos_ref[...], sin_ref[...]
        for block in range(acc_ref.shape[1] // HD):
            cols = slice(block * HD, (block + 1) * HD)
            done = acc_ref[:, cols]
            if block < turned:
                done = done * cosine + pltpu.roll(done, HD // 2, 1) * sine
            done = done.astype(out_ref.dtype)
            for at, mask, row in places:
                dest = pl.multiple_of((info_ref[0] ^ mask) * (SUB * COLOURS) + row, SUB)
                out_ref[pl.ds(dest, SUB), cols] = done[at : at + SUB]


def project(info, xs, weight, tables, turned, places, apart, cols=None, first=0):
    features = xs[0].shape[1]
    total = sum(x.shape[0] for x in xs)
    cols = cols or weight.shape[1]
    block = features // 8
    whole = lambda k, s: (0, 0)
    there = (lambda k, s: (0, s[1] ^ k)) if apart else (lambda k, s: (0, k))
    specs = [pl.BlockSpec((x.shape[0], block), there) for x in xs]
    specs += [pl.BlockSpec((block, cols), lambda k, s: (k, first))]
    specs += [pl.BlockSpec((total, HD), whole)] * 2
    return pl.pallas_call(
        functools.partial(project_kernel, len(xs), turned, places),
        grid_spec=pltpu.PrefetchScalarGridSpec(
            num_scalar_prefetch=1,
            grid=(features // block,),
            in_specs=specs,
            out_specs=pl.BlockSpec((total, cols), whole),
            scratch_shapes=[pltpu.VMEM((total, cols), jnp.float32)],
        ),
        out_shape=jax.ShapeDtypeStruct((total, cols), jnp.bfloat16),
        compiler_params=pltpu.CompilerParams(vmem_limit_bytes=40 * MIB),
        cost_estimate=pl.CostEstimate(
            flops=2 * total * features * cols,
            bytes_accessed=2 * features * (total + cols),
            transcendentals=0,
        ),
        name="project",
        interpret=INTERPRET,
    )(info, *xs, weight, *tables)


def attention_kernel(keys, docs, info_ref, *refs):
    q_refs, (kv_ref, o_ref, acc_ref) = refs[:-3], refs[-3:]
    here = q_refs[0].shape[0]
    heads = sum(ref.shape[1] for ref in q_refs) // HD
    per = q_refs[0].shape[1] // HD
    run = here // 2
    part = kv_ref.shape[0] // 8
    side = info_ref[1]
    left, right = side, 3 - side
    base = info_ref[2] + pl.program_id(0) * 2 * here
    lane = lax.broadcasted_iota(jnp.int32, (1, here), 1)
    rows = base + lane + jnp.where(lane < run, left * run, right * run - run)
    first = base + left * run
    last = base + right * run + run - 1
    low = jnp.zeros((1, here), jnp.int32)
    low_first = jnp.int32(0)
    low_last = jnp.int32(0)
    for d in range(docs):
        end = info_ref[3 + d]
        low = jnp.where(rows >= end, jnp.maximum(low, end), low)
        low_first = jnp.where(first >= end, jnp.maximum(low_first, end), low_first)
        low_last = jnp.where(last >= end, jnp.maximum(low_last, end), low_last)
    rows = jnp.concatenate([rows, rows], axis=1)
    low = jnp.concatenate([low, low], axis=1)
    factor = HD ** (-0.5) * math.log2(math.e)
    acc_ref[...] = jnp.zeros_like(acc_ref)
    tiles = heads // 2
    width = 2 * here
    at_key = lax.broadcasted_iota(jnp.int32, (keys, 1), 0)
    late = (at_key >> 6) & 1
    block = jnp.where(at_key < keys // 2, 3 * late, 1 + late)
    offset = ((at_key >> 7) & 1) * 256 + block * 64 + (at_key & 63)

    def head(h):
        return q_refs[h // per][:, h % per * HD : (h % per + 1) * HD]

    def step(masked, i, state):
        begin = i * keys
        apart = (begin // (2 * part)) ^ info_ref[0]
        start = ((apart >> 1) + (apart & 1) * 2) * 2 * part + begin % (2 * part) // 2
        at = [pl.multiple_of(start + (other ^ side) * part, keys // 2) for other in range(2)]
        key = jnp.concatenate([kv_ref[pl.ds(a, keys // 2), :HD] for a in at], axis=0)
        value = jnp.concatenate([kv_ref[pl.ds(a, keys // 2), HD:] for a in at], axis=0)
        if masked:
            index = begin + offset
            visible = (index >= low) & (index <= rows)
        scored = [
            lax.dot_general(
                key,
                jnp.concatenate([head(2 * h), head(2 * h + 1)], axis=0),
                (((1,), (1,)), ((), ())),
                preferred_element_type=jnp.float32,
            )
            for h in range(tiles)
        ]
        out = []
        for h in range(tiles):
            top, total = state[h]
            scores = scored[h] * factor
            if masked:
                scores = jnp.where(visible, scores, jnp.float32(-1e30))
            new = jnp.maximum(top, jnp.max(scores, axis=0, keepdims=True))
            keep = jnp.exp2(top - new)
            expd = jnp.exp2(scores - new)
            total = total * keep + jnp.sum(expd, axis=0, keepdims=True)
            acc_ref[h] = acc_ref[h] * keep + lax.dot_general(
                value, expd.astype(jnp.bfloat16), (((0,), (0,)), ((), ())), preferred_element_type=jnp.float32
            )
            out.append((new, total))
        return tuple(out)

    state = tuple((jnp.full((1, width), -1e30, jnp.float32), jnp.zeros((1, width), jnp.float32)) for _ in range(tiles))
    begin, end = low_first // keys, last // keys + 1
    clear = jnp.minimum((low_last + keys - 1) // keys, end)
    edge = jnp.maximum(first // keys, clear)
    state = lax.fori_loop(begin, clear, functools.partial(step, True), state)
    state = lax.fori_loop(clear, edge, functools.partial(step, False), state)
    state = lax.fori_loop(edge, end, functools.partial(step, True), state)
    for h in range(tiles):
        done = (acc_ref[h] / state[h][1]).T.astype(o_ref.dtype)
        for p in range(2):
            o_ref[:, (2 * h + p) * HD : (2 * h + p + 1) * HD] = done[p * here : (p + 1) * here]


def attention(info, qs, kv, docs, here=128, keys=512):
    rows = qs[0].shape[0]
    cols = sum(q.shape[1] for q in qs)
    return pl.pallas_call(
        functools.partial(attention_kernel, keys, docs),
        grid_spec=pltpu.PrefetchScalarGridSpec(
            num_scalar_prefetch=1,
            grid=(rows // here,),
            in_specs=[pl.BlockSpec((here, q.shape[1]), lambda i, s: (i, 0)) for q in qs]
            + [pl.BlockSpec(kv.shape, lambda i, s: (0, 0))],
            out_specs=pl.BlockSpec((here, cols), lambda i, s: (i, 0)),
            scratch_shapes=[pltpu.VMEM((cols // HD // 2, HD, 2 * here), jnp.float32)],
        ),
        out_shape=jax.ShapeDtypeStruct((rows, cols), jnp.bfloat16),
        compiler_params=pltpu.CompilerParams(vmem_limit_bytes=40 * MIB),
        cost_estimate=pl.CostEstimate(
            flops=4 * rows * cols * 2048, bytes_accessed=8 * MIB, transcendentals=rows * cols // HD * 2048
        ),
        name="attention",
        interpret=INTERPRET,
    )(info, *qs, kv)


def outward_kernel(masks, info_ref, h_ref, w_ref, other_ref, keep_ref, send_ref, moved_ref):
    rows = h_ref.shape[0] // len(masks)

    @pl.when(pl.program_id(0) == 0)
    def _():
        for place, mask in enumerate(masks):
            source = pl.multiple_of((info_ref[0] ^ mask) * rows, rows)
            moved_ref[place * rows : (place + 1) * rows, :] = h_ref[pl.ds(source, rows), :]

    half = keep_ref.shape[0]
    inner = w_ref.shape[0]
    done = jnp.dot(moved_ref[:, :inner], w_ref[...], preferred_element_type=jnp.float32) + jnp.dot(
        moved_ref[:, inner:], other_ref[...], preferred_element_type=jnp.float32
    )
    done = done.astype(keep_ref.dtype)
    keep_ref[...] = done[:half]
    send_ref[...] = done[half:]


def outward(info, heads_out, weight, other, colour, masks):
    rows, inner = heads_out.shape
    cols = weight.shape[1] // COLOURS
    block = weight.shape[1] // 16
    steps = cols // block
    half = jax.ShapeDtypeStruct((rows // 2, cols), jnp.bfloat16)

    def theirs(n, s):
        at = colour * steps + n
        return ((at // 2 ^ s[1]) * 2 + at % 2, 0)

    return pl.pallas_call(
        functools.partial(outward_kernel, masks),
        grid_spec=pltpu.PrefetchScalarGridSpec(
            num_scalar_prefetch=1,
            grid=(steps,),
            in_specs=[
                pl.BlockSpec((rows, inner), lambda n, s: (0, 0)),
                pl.BlockSpec((inner // 2, block), lambda n, s: (0, colour * steps + n)),
                pl.BlockSpec((inner // 2, block), theirs),
            ],
            out_specs=[pl.BlockSpec((rows // 2, block), lambda n, s: (0, n))] * 2,
            scratch_shapes=[pltpu.VMEM((rows, inner), jnp.bfloat16)],
        ),
        out_shape=[half, half],
        compiler_params=pltpu.CompilerParams(vmem_limit_bytes=24 * MIB),
        cost_estimate=pl.CostEstimate(
            flops=2 * rows * inner * cols, bytes_accessed=2 * (rows * inner + inner * cols + rows * cols), transcendentals=0
        ),
        name="outward",
        interpret=INTERPRET,
    )(info, heads_out, weight, other)


def local(hidden_in, norm_gain, q_weight, kv_weight, out_weight, doc_lengths):
    tok_rows = hidden_in.shape[0]
    n_tp = lax.axis_size("tp")
    half = n_tp // 2
    tp_index = lax.axis_index("tp")
    ctx_index = lax.axis_index("ctx")
    column = ctx_index * lax.axis_size("dp") + lax.axis_index("dp")
    ends = jnp.cumsum(doc_lengths).astype(jnp.int32)
    first_row = ctx_index * tok_rows * n_tp

    depth = q_weight.shape[0] // 8
    kv_piece = lax.dynamic_slice_in_dim(kv_weight, column * depth, depth, 0)
    same = [(i, 2 * i) for i in range(half)] + [(half + i, 2 * i + 1) for i in range(half)]
    other = [(i, 2 * i + 1) for i in range(half)] + [(half + i, 2 * i) for i in range(half)]
    one = lax.ppermute(kv_piece, "tp", same)
    two = lax.ppermute(kv_piece, "tp", other)
    even = tp_index % 2 == 0
    kv_piece = jnp.concatenate([jnp.where(even, one, two), jnp.where(even, two, one)], axis=1)
    q_piece = swap(lax.dynamic_slice_in_dim(q_weight, column * depth, depth, 0), "tp", 1)
    width = out_weight.shape[1] // 16
    out_piece = lax.dynamic_slice_in_dim(out_weight, column * 2 * width, 2 * width, 1)
    out_piece = swap(jnp.concatenate([out_piece[:, :width], out_piece[:, width:]], axis=0), "tp", 1)

    x = hidden_in.astype(jnp.float32)
    normed = (
        x * lax.rsqrt(jnp.mean(x * x, axis=1, keepdims=True) + 1e-05) * norm_gain[None, :]
    ).astype(jnp.bfloat16)
    held = [normed[c * SUB : (c + 1) * SUB] for c in range(COLOURS)]
    steps = len(GATHER[0])
    for step in range(steps - 1):
        held = [jnp.concatenate([s, swap(s, "tp", GATHER[c][step])], axis=0) for c, s in enumerate(held)]
    late = [swap(s, "tp", GATHER[c][steps - 1]) for c, s in enumerate(held)]

    kv_there, kv_far = column_gather(kv_piece)
    q_there, q_far = column_gather(after(q_piece, kv_far))
    out_there, _ = column_gather(after(out_piece, q_far))

    starts, places = [], []
    for part in range(2):
        for c, order in enumerate(GATHER):
            for p in range(half // 2):
                mask = mask_of(order, part * half // 2 + p)
                starts.append((tp_index ^ mask) * tok_rows + c * SUB)
                places.append((len(places) * SUB, place_of(mask), c * SUB))
    places = tuple(places)
    positions = first_row + (jnp.stack(starts)[:, None] + jnp.arange(SUB)[None, :]).reshape(-1)
    tables = rope_tables(positions.astype(jnp.int32), ends)
    info = jnp.stack([tp_index >> 1, column]).astype(jnp.int32)

    xs = [*held, *late]
    kv_mine = project(info, xs, kv_there, tables, 1, places, True)
    kv_chip = jnp.concatenate(
        [
            kv_mine,
            swap(kv_mine, "tp", 1),
            swap(kv_mine, "ctx", 2),
            swap(kv_mine, ("ctx", "tp"), 2 * n_tp + 1),
        ],
        axis=0,
    )
    kv_all = jnp.concatenate([kv_chip, swap(kv_chip, "ctx", 1)], axis=0)
    heads_here = q_weight.shape[1] // HD
    mine = project(info, xs, q_weight, tables, heads_here, places, False)
    theirs = project(info, xs, q_there, tables, heads_here, places, True)

    side = (tp_index ^ (tp_index >> 1)) & 1
    where = jnp.concatenate([jnp.stack([ctx_index, side, first_row]).astype(jnp.int32), ends])
    heads_out = attention(where, [mine, theirs], kv_all, doc_lengths.shape[0])

    kept, sent = [], []
    for c, order in enumerate(REDUCE):
        masks = tuple(place_of(mask_of(order[::-1], p)) for p in range(half))
        keep, send = outward(info, heads_out, out_weight, out_there, c, masks)
        kept.append(keep)
        sent.append(send)
    for step in range(steps):
        arrived = [swap(s, "tp", REDUCE[c][step]) for c, s in enumerate(sent)]
        sums = [(k.astype(jnp.float32) + a.astype(jnp.float32)).astype(jnp.bfloat16) for k, a in zip(kept, arrived)]
        rows = sums[0].shape[0] // 2
        kept = [s[:rows] for s in sums]
        sent = [s[rows:] for s in sums]
    return jnp.concatenate(sums, axis=1)


def solution(mesh):
    placed = (
        P(("dp", "ctx", "tp"), None),
        P(),
        P(None, "tp"),
        P(None, "tp"),
        P("tp", None),
        P("dp"),
    )
    return jax.shard_map(
        local, mesh=mesh, in_specs=placed, out_specs=P(("dp", "ctx", "tp"), None), check_vma=False
    )
```
